32 devices in a mesh: groups: 2 (over y), seq: 4 (over z), eta: 2 (over x), rep: 2 (over core).
Axes of the slice: x: 2, y: 2, z: 4, core: 2. Of those that a mesh axis runs over, the one named last changes fastest.
Arguments:
- features: bfloat16 [4, 2048, 2048], P(('groups', 'eta'), 'seq', 'rep'), parts along dimension 0, may hold values from -6 to 6
- step_sizes: float32 [4, 2048, 32], P(('groups', 'eta'), 'seq', 'rep'), parts along dimension 0, may hold values from 0 to 2
- log_decay: float32 [4, 2048, 32], P(('groups', 'eta'), 'seq', 'rep'), parts along dimension 0, may hold values from -2 to 0
- state_in: bfloat16 [4, 2048, 128], P(('groups', 'eta'), 'seq'), parts along dimension 0, may hold values from -6 to 6
- state_out: bfloat16 [4, 2048, 128], P(('groups', 'eta'), 'seq'), parts along dimension 0, may hold values from -0.5 to 0.5
- skip_gain: float32 [32], P('rep'), may hold values from 0.5 to 1.5
- kernels: bfloat16 [4, 128, 128], replicated, may hold values from -0.5 to 0.5
- edge_lists: int32 [4, 4, 16, 4], P('groups', 'seq'), parts along dimension 0, may hold values from 0 to 3, as said below
- edge_counts: int32 [4, 4], P('groups', 'seq'), parts along dimension 0, may hold values from 1 to 16, as said below
- cotangent: bfloat16 [4, 2048, 2048], P(('groups', 'eta'), 'seq', 'rep'), parts along dimension 0, may hold values from -6 to 6
Outputs:
- layer_out: bfloat16 [4, 2048, 2048], P(('groups', 'eta'), 'seq', 'rep'), parts along dimension 0
- grad_features: bfloat16 [4, 2048, 2048], P(('groups', 'eta'), 'seq', 'rep'), parts along dimension 0
The draws below stay inside these ranges and needn't reach their ends.
There are 2 independent parts, one for each index of `groups`. The reference program is written for one: setup_inputs(seed, part) draws one part's arguments, and reference() takes and returns one part's arrays. A program takes and returns all parts, laid end to end along the dimension named above; an argument that names none is the same for every part. Nothing has to cross between parts.
Inputs may be any that keep to these rules, and one draw needn't show every extreme that they name: `edge_lists`: rows are (source band offset 0, 1 or 2 for the band below, the same band or the band above; source block; target block; type). The used rows of a segment never name a band outside 0 to 1, and no two rows of a segment share their first three fields. `edge_counts`: every band's segments use between one and all 16 slots.
All inputs are finite; a program needn't handle non-finite values.
Results may differ from the reference program's by a relative error of at most 0.0053.
Values may be sent and summed in bfloat16 or wider, within the bound.
No kernel may reach another device: no remote copies, remote signals or barrier semaphores. Data moves between devices by JAX's collectives and lax.ppermute only.
A program may use at most 128 MiB of HBM per device.

```python
import math
import jax
import jax.numpy as jnp
from jax import lax

H = 32
P_SIZE = 64
N = 128
CH = 128
BLOCK = 128
TYPES = 4
TOK_DEV = 512
ETA_BAND_COUNT = 2
SEGS = 4
BAND_HIT_LENGTH = 2048
NB = 4
E_CAP = 16


def draw_step_sizes(key, part):
    full_shape = (ETA_BAND_COUNT, BAND_HIT_LENGTH, H)
    base_draw = jnp.exp(jax.random.uniform(key, full_shape, jnp.float32, math.log(0.5), math.log(2.0)))
    return base_draw / math.sqrt(BAND_HIT_LENGTH)


def draw_log_decay(key, part):
    random_subkeys = jax.random.split(key, 7)
    fast_share = 0.5
    is_fast = jax.random.uniform(random_subkeys[0], (ETA_BAND_COUNT, 1, H), jnp.float32) < fast_share
    fast_rate = jnp.exp(jax.random.uniform(random_subkeys[1], (ETA_BAND_COUNT, 1, H), jnp.float32, math.log(1.0 / 50.0), math.log(1.0 / 30.0)))
    slow_rate = jnp.exp(jax.random.uniform(random_subkeys[2], (ETA_BAND_COUNT, 1, H), jnp.float32, math.log(0.05), math.log(0.2))) / BAND_HIT_LENGTH
    per_head_rate = jnp.where(is_fast, fast_rate, slow_rate)
    detector_factor = jnp.exp(jax.random.uniform(random_subkeys[3], (ETA_BAND_COUNT, SEGS, 1, 1), jnp.float32, math.log(0.5), math.log(2.0)))
    detector_factor = jnp.broadcast_to(detector_factor, (ETA_BAND_COUNT, SEGS, TOK_DEV, 1)).reshape(ETA_BAND_COUNT, BAND_HIT_LENGTH, 1)
    jitter_amount = jnp.exp(jax.random.uniform(random_subkeys[4], (ETA_BAND_COUNT, BAND_HIT_LENGTH, H), jnp.float32, math.log(0.5), math.log(2.0)))
    spike_position = jax.random.randint(random_subkeys[5], (ETA_BAND_COUNT, 2), 0, BAND_HIT_LENGTH)
    spike_length = jax.random.uniform(random_subkeys[6], (ETA_BAND_COUNT, 2), jnp.float32, 0.22, 0.69)
    hit_positions = jnp.arange(BAND_HIT_LENGTH, dtype=jnp.int32)[None, :, None]
    spike_loss = jnp.sum(jnp.where(hit_positions == spike_position[:, None, :], spike_length[:, None, :], 0.0), axis=2)
    return -(per_head_rate * detector_factor * jitter_amount) - spike_loss[:, :, None]


def edge_tables(key):
    folded = jax.random.fold_in(key, 11)
    random_subkeys = jax.random.split(folded, 3)
    pairs = 3 * NB * NB
    candidates = jnp.arange(pairs, dtype=jnp.int32)[None, None, :]
    band_ids = jnp.arange(ETA_BAND_COUNT, dtype=jnp.int32)[:, None, None]
    rel_band = candidates // (NB * NB)
    invalid = (band_ids == 0) & (rel_band == 0) | (band_ids == ETA_BAND_COUNT - 1) & (rel_band == 2)
    scores_int = jax.random.randint(random_subkeys[0], (ETA_BAND_COUNT, SEGS, pairs), 0, 2 ** 20) * pairs + candidates + jnp.where(invalid, 2 ** 30, 0)
    ranked = jnp.argsort(scores_int, axis=-1)[:, :, :E_CAP].astype(jnp.int32)
    src_rel = ranked // (NB * NB)
    src_block = ranked // NB % NB
    dst_block = ranked % NB
    kinds = jax.random.randint(random_subkeys[1], (ETA_BAND_COUNT, SEGS, E_CAP), 0, TYPES)
    edge_table = jnp.stack([src_rel, src_block, dst_block, kinds], axis=-1).astype(jnp.int32)
    counts = jax.random.randint(random_subkeys[2], (ETA_BAND_COUNT, SEGS), 1, E_CAP + 1)
    counts = jnp.where(jnp.arange(ETA_BAND_COUNT, dtype=jnp.int32)[:, None] == ETA_BAND_COUNT // 2, E_CAP, counts).astype(jnp.int32)
    return (edge_table, counts)


def draw_edge_lists(key, part):
    return edge_tables(key)[0]


def draw_edge_counts(key, part):
    return edge_tables(key)[1]


def levels(stream_key, shape, cuts, least, largest):
    level = 1.0
    for dim, parts in cuts:
        draws = jax.random.uniform(jax.random.fold_in(jax.random.fold_in(stream_key, 6), dim), (parts,), jnp.float32, least / len(cuts), largest / len(cuts))
        level = level * jnp.repeat(jnp.exp(draws), shape[dim] // parts).reshape((-1,) + (1,) * (len(shape) - 1 - dim))
    return level


def gaussian(rng, shape, deviation, bound, cuts=(), kind=jnp.bfloat16):
    factor_of = levels(rng, shape, cuts, -0.22, 0.18) if cuts else 1.0
    drawn = jax.random.normal(rng, shape, jnp.float32) * deviation * factor_of
    return jnp.minimum(jnp.maximum(drawn, -bound), bound).astype(kind)


def setup_inputs(seed: int = 0, part: int = 0) -> dict:
    streams_of = jax.random.split(jax.random.key(seed), 11)
    own_keys = jax.random.split(jax.random.fold_in(streams_of[10], part), 11)
    return {
        "features": gaussian(own_keys[0], (ETA_BAND_COUNT, BAND_HIT_LENGTH, H * P_SIZE), 1.0, 6.0, ((0, 2), (1, 4), (2, 2))),
        "step_sizes": draw_step_sizes(jax.random.fold_in(jax.random.fold_in(streams_of[10], part), 71), part),
        "log_decay": draw_log_decay(jax.random.fold_in(jax.random.fold_in(streams_of[10], part), 71), part),
        "state_in": gaussian(own_keys[3], (ETA_BAND_COUNT, BAND_HIT_LENGTH, N), 1.0, 6.0, ((0, 2), (1, 4))),
        "state_out": gaussian(own_keys[4], (ETA_BAND_COUNT, BAND_HIT_LENGTH, N), N ** -0.5, 0.5, ((0, 2), (1, 4))),
        "skip_gain": jnp.clip(0.5 + 1.0 * jax.random.uniform(streams_of[5], (H,), jnp.float32) ** levels(streams_of[5], (H,), ((0, 2),), -0.2, 0.2), 0.5, 1.5),
        "kernels": gaussian(streams_of[6], (TYPES, BLOCK, BLOCK), BLOCK ** -0.5, 0.5),
        "edge_lists": draw_edge_lists(jax.random.fold_in(jax.random.fold_in(streams_of[10], part), 71), part),
        "edge_counts": draw_edge_counts(jax.random.fold_in(jax.random.fold_in(streams_of[10], part), 71), part),
        "cotangent": gaussian(own_keys[9], (ETA_BAND_COUNT, BAND_HIT_LENGTH, H * P_SIZE), 1.0, 6.0, ((0, 2), (1, 4), (2, 2))),
    }


highest_prec = lax.Precision.HIGHEST


def span_parts(log_span, step_span, in_span, out_span):
    cum_log = jnp.cumsum(log_span, axis=0)
    span_len = cum_log.shape[0]
    row_ids = lax.broadcasted_iota(jnp.int32, (span_len, span_len), 0)
    col_ids = lax.broadcasted_iota(jnp.int32, (span_len, span_len), 1)
    causal = (row_ids >= col_ids)[None]
    spread = jnp.transpose(cum_log)
    differ = spread[:, :, None] - spread[:, None, :]
    decays = jnp.where(causal, jnp.exp(jnp.where(causal, differ, 0.0)), 0.0)
    scores = jnp.dot(out_span, in_span.T, preferred_element_type=jnp.float32)
    weights = (scores[None] * decays * jnp.transpose(step_span)[:, None, :]).astype(jnp.bfloat16)
    rate_terms = jnp.exp(cum_log[-1][None, :] - cum_log) * step_span
    return cum_log, weights, rate_terms


def span_forward(feat_span, skip_gain, cum_log, weights, rate_terms, in_span, out_span, state_now):
    feat_wide = feat_span.astype(jnp.float32)
    inside = jnp.einsum('hij,jhp->ihp', weights.astype(jnp.float32), feat_wide)
    carried = jnp.exp(cum_log)[:, :, None] * jnp.einsum('in,hpn->ihp', out_span.astype(jnp.float32), state_now, precision=highest_prec)
    output = inside + carried + skip_gain[None, :, None] * feat_wide
    scaled = (rate_terms[:, :, None] * feat_wide).astype(jnp.bfloat16)
    state_next = jnp.exp(cum_log[-1])[:, None, None] * state_now + jnp.einsum('jhp,jn->hpn', scaled.astype(jnp.float32), in_span.astype(jnp.float32))
    return output, state_next


def span_backward(grad_span, skip_gain, cum_log, weights, rate_terms, in_span, out_span, adjoint_now):
    grad_wide = grad_span.astype(jnp.float32)
    through = jnp.einsum('hij,ihp->jhp', weights.astype(jnp.float32), grad_wide)
    from_state = rate_terms[:, :, None] * jnp.einsum('jn,hpn->jhp', in_span.astype(jnp.float32), adjoint_now, precision=highest_prec)
    grad_feat = through + skip_gain[None, :, None] * grad_wide + from_state
    adjoint_prev = jnp.exp(cum_log[-1])[:, None, None] * adjoint_now + jnp.einsum('ihp,in->hpn', jnp.exp(cum_log)[:, :, None] * grad_wide, out_span.astype(jnp.float32), precision=highest_prec)
    return grad_feat, adjoint_prev


def band_forward(band_parts, skip_gain):
    features, step_sizes, log_decay, state_in, state_out = band_parts
    span_count = BAND_HIT_LENGTH // CH
    feats = features.reshape(span_count, CH, H, P_SIZE)
    steps_c = step_sizes.reshape(span_count, CH, H)
    logs_c = log_decay.reshape(span_count, CH, H)
    ins_c = state_in.reshape(span_count, CH, N)
    outs_c = state_out.reshape(span_count, CH, N)

    def advance(state_now, pieces):
        feat_span, step_span, log_span, in_span, out_span = pieces
        cum_log, weights, rate_terms = span_parts(log_span, step_span, in_span, out_span)
        output, state_next = span_forward(feat_span, skip_gain, cum_log, weights, rate_terms, in_span, out_span, state_now)
        return state_next, output

    _, outputs = lax.scan(advance, jnp.zeros((H, P_SIZE, N), jnp.float32), (feats, steps_c, logs_c, ins_c, outs_c))
    return outputs.reshape(BAND_HIT_LENGTH, H * P_SIZE).astype(jnp.bfloat16)


def band_backward(band_parts, skip_gain):
    ssd_grad, step_sizes, log_decay, state_in, state_out = band_parts
    span_count = BAND_HIT_LENGTH // CH
    grads_c = ssd_grad.reshape(span_count, CH, H, P_SIZE)
    steps_c = step_sizes.reshape(span_count, CH, H)
    logs_c = log_decay.reshape(span_count, CH, H)
    ins_c = state_in.reshape(span_count, CH, N)
    outs_c = state_out.reshape(span_count, CH, N)

    def retreat(adjoint_now, pieces):
        grad_span, step_span, log_span, in_span, out_span = pieces
        cum_log, weights, rate_terms = span_parts(log_span, step_span, in_span, out_span)
        grad_feat, adjoint_prev = span_backward(grad_span, skip_gain, cum_log, weights, rate_terms, in_span, out_span, adjoint_now)
        return adjoint_prev, grad_feat

    _, grads = lax.scan(retreat, jnp.zeros((H, P_SIZE, N), jnp.float32), (grads_c, steps_c, logs_c, ins_c, outs_c), reverse=True)
    return grads.reshape(BAND_HIT_LENGTH, H * P_SIZE).astype(jnp.bfloat16)


def graph_forward(ssd_out, kernels, edge_lists, edge_counts):
    blocks = ssd_out.reshape(ETA_BAND_COUNT, SEGS, NB, BLOCK, H * P_SIZE)
    band_ids = jnp.broadcast_to(jnp.arange(ETA_BAND_COUNT, dtype=jnp.int32)[:, None], (ETA_BAND_COUNT, SEGS))
    seg_ids = jnp.broadcast_to(jnp.arange(SEGS, dtype=jnp.int32)[None, :], (ETA_BAND_COUNT, SEGS))

    def add_edge(message, edge_slot):
        edge_row = edge_lists[:, :, edge_slot]
        is_live = (edge_slot < edge_counts).astype(jnp.float32)
        src_band = jnp.clip(band_ids + edge_row[..., 0] - 1, 0, ETA_BAND_COUNT - 1)
        source = blocks[src_band, seg_ids, edge_row[..., 1]]
        kernel = kernels[edge_row[..., 3]]
        contrib = jnp.einsum('bsij,bsjd->bsid', kernel.astype(jnp.float32), source.astype(jnp.float32))
        contrib = contrib * is_live[:, :, None, None]
        message = message.at[band_ids, seg_ids, edge_row[..., 2]].add(contrib)
        return message, None

    empty = jnp.zeros((ETA_BAND_COUNT, SEGS, NB, BLOCK, H * P_SIZE), jnp.float32)
    message, _ = lax.scan(add_edge, empty, jnp.arange(E_CAP, dtype=jnp.int32))
    return message.reshape(ETA_BAND_COUNT, BAND_HIT_LENGTH, H * P_SIZE)


def graph_backward(cotangent, kernels, edge_lists, edge_counts):
    blocks = cotangent.reshape(ETA_BAND_COUNT, SEGS, NB, BLOCK, H * P_SIZE)
    band_ids = jnp.broadcast_to(jnp.arange(ETA_BAND_COUNT, dtype=jnp.int32)[:, None], (ETA_BAND_COUNT, SEGS))
    seg_ids = jnp.broadcast_to(jnp.arange(SEGS, dtype=jnp.int32)[None, :], (ETA_BAND_COUNT, SEGS))

    def add_edge(back_terms, edge_slot):
        edge_row = edge_lists[:, :, edge_slot]
        is_live = (edge_slot < edge_counts).astype(jnp.float32)
        src_band = jnp.clip(band_ids + edge_row[..., 0] - 1, 0, ETA_BAND_COUNT - 1)
        target = blocks[band_ids, seg_ids, edge_row[..., 2]]
        kernel = kernels[edge_row[..., 3]]
        contrib = jnp.einsum('bsji,bsjd->bsid', kernel.astype(jnp.float32), target.astype(jnp.float32))
        contrib = contrib * is_live[:, :, None, None]
        back_terms = back_terms.at[src_band, seg_ids, edge_row[..., 1]].add(contrib)
        return back_terms, None

    empty = jnp.zeros((ETA_BAND_COUNT, SEGS, NB, BLOCK, H * P_SIZE), jnp.float32)
    back_terms, _ = lax.scan(add_edge, empty, jnp.arange(E_CAP, dtype=jnp.int32))
    return back_terms.reshape(ETA_BAND_COUNT, BAND_HIT_LENGTH, H * P_SIZE)


def reference(features, step_sizes, log_decay, state_in, state_out, skip_gain, kernels, edge_lists, edge_counts, cotangent):
    def run_forward(band_parts):
        return band_forward(band_parts, skip_gain)

    def run_backward(band_parts):
        return band_backward(band_parts, skip_gain)

    ssd_out = lax.map(run_forward, (features, step_sizes, log_decay, state_in, state_out))
    message = graph_forward(ssd_out, kernels, edge_lists, edge_counts)
    layer_out = (ssd_out.astype(jnp.float32) + message).astype(jnp.bfloat16)
    back_terms = graph_backward(cotangent, kernels, edge_lists, edge_counts)
    ssd_grad = (cotangent.astype(jnp.float32) + back_terms).astype(jnp.bfloat16)
    grad_features = lax.map(run_backward, (ssd_grad, step_sizes, log_decay, state_in, state_out))
    return layer_out, grad_features
```

```python
import jax
import jax.numpy as jnp
from jax import lax
from jax.experimental import pallas as pl
from jax.experimental.pallas import tpu as pltpu
from jax.sharding import PartitionSpec as P

CH = 128
BLOCK = 128
PAD = 16
GROUPS = 2

F32 = jnp.float32
BF16 = jnp.bfloat16


def dot(a, b):
    return jnp.dot(a, b, preferred_element_type=F32)


def dot_rows(a, b):
    return lax.dot_general(a, b, (((0,), (0,)), ((), ())), preferred_element_type=F32)


def pieces(x, count):
    out = []
    for _ in range(count):
        part = x.astype(BF16)
        out.append(part)
        x = x - part.astype(F32)
    return out


def spread_matrix(heads, width, first, head_width):
    row = lax.broadcasted_iota(jnp.int32, (heads, width), 0)
    col = lax.broadcasted_iota(jnp.int32, (heads, width), 1)
    low = (row - first) * head_width
    return ((col >= low) & (col < low + head_width)).astype(F32).astype(BF16)


def spread(x, matrix):
    high, low = pieces(x, 2)
    return dot(high, matrix) + dot(low, matrix)


def run(kernel, outs, args, in_specs=None, out_specs=None, aliases=None, us=1.0, name=None, **kw):
    vmem = pl.BlockSpec(memory_space=pltpu.VMEM)
    return pl.pallas_call(
        kernel,
        out_shape=outs,
        in_specs=in_specs or [vmem] * len(args),
        out_specs=out_specs or jax.tree.map(lambda _: vmem, outs),
        input_output_aliases=aliases or {},
        cost_estimate=pl.CostEstimate(
            flops=0, bytes_accessed=int(us * 3.0e6), transcendentals=0
        ),
        name=name,
        **kw,
    )(*args)


def shape(dims, kind):
    return jax.ShapeDtypeStruct(dims, kind)


class Plan:
    def __init__(self, tok, width, heads, state):
        self.tok, self.width, self.heads, self.state = tok, width, heads, state
        self.head_width = width // heads
        self.spans = tok // CH
        self.groups = GROUPS
        self.part = width // GROUPS
        self.group_heads = heads // GROUPS
        self.blocks = tok // BLOCK


def pack_tail(total, part):
    tail = jnp.concatenate([p.astype(F32) for p in pieces(total, 3)], axis=0)
    return jnp.concatenate([tail, jnp.zeros((PAD - 3, part), F32)], axis=0).astype(BF16)


def unpack_tail(ref, rows):
    tail = ref[rows : rows + PAD, :].astype(F32)
    return tail[0:1] + tail[1:2] + tail[2:3]


def states_body(plan):
    spans, heads, part, n = plan.spans, plan.heads, plan.part, plan.state

    def kernel(feat, step, log, into, cum_out, *outs):
        rows = lax.broadcasted_iota(jnp.int32, (CH, CH), 0)
        cols = lax.broadcasted_iota(jnp.int32, (CH, CH), 1)
        lower = (rows >= cols).astype(F32).astype(BF16)
        rates, tots = [], []
        for k in range(spans):
            at = slice(k * CH, (k + 1) * CH)
            cum = sum(dot(lower, p) for p in pieces(log[at, :], 3))
            cum_out[at, :] = cum
            tots.append(cum[CH - 1 : CH])
            rates.append(jnp.exp(cum[CH - 1 : CH] - cum) * step[at, :])
        tot = jnp.concatenate(tots + [sum(tots)] * (8 - spans), axis=0)
        for g in range(plan.groups):
            prefix_out, packed = outs[2 * g], outs[2 * g + 1]
            lanes = slice(g * part, (g + 1) * part)
            matrix = spread_matrix(heads, part, g * plan.group_heads, plan.head_width)
            high, mid, low = pieces(tot, 3)
            tot_wide = dot(high, matrix) + dot(mid, matrix) + dot(low, matrix)
            state = None
            for k in range(spans):
                at = slice(k * CH, (k + 1) * CH)
                scaled = (spread(rates[k], matrix) * feat[at, lanes].astype(F32)).astype(BF16)
                fresh = dot_rows(into[at, :], scaled)
                state = fresh if state is None else jnp.exp(tot_wide[k : k + 1]) * state + fresh
                if k + 1 < spans:
                    prefix_out[k] = state.astype(BF16)
            packed[:n, :] = state.astype(BF16)
            packed[n:, :] = pack_tail(tot_wide[spans : spans + 1], part)

    return kernel


def weights_body(plan):
    spans, heads, part, n, pw = plan.spans, plan.heads, plan.part, plan.state, plan.head_width

    def kernel(feat, step, cum_ref, into, outof, skip, *refs):
        prefixes = refs[: plan.groups]
        flipped = refs[plan.groups]
        partials = refs[plan.groups + 1 :]
        rows = lax.broadcasted_iota(jnp.int32, (CH, CH), 0)
        cols = lax.broadcasted_iota(jnp.int32, (CH, CH), 1)
        causal = rows >= cols
        left = cols < pw
        zero = jnp.zeros((CH, CH), BF16)
        for k in range(spans):
            at = slice(k * CH, (k + 1) * CH)
            score = lax.dot_general(
                outof[at, :], into[at, :], (((1,), (1,)), ((), ())), preferred_element_type=F32
            )
            score = jnp.where(causal, score, 0.0)
            cum = cum_ref[at, :]
            both = jnp.concatenate(
                [cum, step[at, :], jnp.zeros((CH, CH - 2 * heads), F32)], axis=1
            )
            turned = both.T
            for g in range(plan.groups):
                base = g * part
                matrix = spread_matrix(heads, part, g * plan.group_heads, pw)
                skip_wide = spread(jnp.broadcast_to(skip[...], (8, heads)), matrix)[0:1]
                rest = skip_wide * feat[at, base : base + part].astype(F32)
                if k > 0:
                    rest += spread(jnp.exp(cum), matrix) * dot(outof[at, :], prefixes[g][k - 1])
                for pair in range(plan.group_heads // 2):
                    lanes = slice(pair * 2 * pw, (pair + 1) * 2 * pw)
                    ws = []
                    for h in (0, 1):
                        head = g * plan.group_heads + 2 * pair + h
                        gap = cum[:, head : head + 1] - turned[head : head + 1, :]
                        decay = jnp.exp(jnp.minimum(gap, 0.0))
                        w = score * decay * turned[heads + head : heads + head + 1, :]
                        w = w.astype(BF16)
                        ws.append(w)
                        where = (g * plan.group_heads // 2 + pair) * 2 * CH
                        flipped[at, where + h * CH : where + (h + 1) * CH] = w.T
                    x = feat[at, base + pair * 2 * pw : base + (pair + 1) * 2 * pw]
                    stacked = jnp.concatenate(
                        [jnp.where(left, x, zero), jnp.where(left, zero, x)], axis=0
                    )
                    inside = dot(jnp.concatenate(ws, axis=1), stacked)
                    partials[g][at, lanes] = inside + rest[:, lanes]

    return kernel


def device_cum(cum_ref, spans):
    out, before = [], None
    for k in range(spans):
        cum = cum_ref[k * CH : (k + 1) * CH, :]
        out.append(cum if before is None else cum + before)
        before = out[-1][CH - 1 : CH]
    return jnp.concatenate(out, axis=0), before


def graph_body(plan, sides):
    tok = plan.tok

    def kernel(edges, counts, kern, cot, fwd_own, *refs):
        fwd_side, back_side = refs[:sides], refs[sides : 2 * sides]
        own_back = refs[2 * sides : 2 * sides + plan.groups]
        back_own = refs[2 * sides + plan.groups]
        bands = lax.axis_size("eta")
        band = lax.axis_index("eta")
        for ref in (fwd_own, back_own, *fwd_side, *back_side):
            ref[...] = jnp.zeros_like(ref)

        def spot(a, b):
            return (
                pl.ds(pl.multiple_of(a * BLOCK, BLOCK), BLOCK),
                pl.ds(pl.multiple_of(b * BLOCK, BLOCK), BLOCK),
            )

        if sides == 1:
            offsets, others = [2 - 2 * band], [1 - band]
        else:
            offsets, others = [0, 2][:sides], [band - 1, band + 1][:sides]

        def own(e, carry):
            off, src, dst, kind = (edges[band, 0, e, f] for f in range(4))
            tile = kern[kind]

            @pl.when(off == 1)
            def _():
                fwd_own[spot(dst, src)] = tile
                back_own[spot(src, dst)] = tile.T

            for s in range(sides):

                @pl.when(off == offsets[s])
                def _():
                    fwd_side[s][spot(dst, src)] = tile

            return carry

        lax.fori_loop(0, counts[band, 0], own, 0)
        for s in range(sides):
            real = (others[s] >= 0) & (others[s] < bands)
            other = jnp.clip(others[s], 0, bands - 1)

            def far(e, carry):
                off, src, dst, kind = (edges[other, 0, e, f] for f in range(4))

                @pl.when(off == 2 - offsets[s])
                def _():
                    back_side[s][spot(src, dst)] = kern[kind].T

                return carry

            lax.fori_loop(0, jnp.where(real, counts[other, 0], 0), far, 0)
        for g in range(plan.groups):
            lanes = slice(g * plan.part, (g + 1) * plan.part)
            own_back[g][...] = dot(back_own[...], cot[:, lanes]) + cot[:, lanes].astype(F32)

    return kernel


def grad_body(plan, sides, g):
    spans, heads, part, n = plan.spans, plan.heads, plan.part, plan.state

    def kernel(own_back, cum_ref, outof, *refs):
        mats, cots = refs[:sides], refs[sides : 2 * sides]
        grad, leaves, packed = refs[2 * sides :]
        matrix = spread_matrix(heads, part, g * plan.group_heads, plan.head_width)
        total = own_back[...]
        for s in range(sides):
            total += dot(mats[s][...], cots[s][...])
        rounded = total.astype(BF16)
        grad[...] = rounded
        tots = jnp.concatenate(
            [cum_ref[(k + 1) * CH - 1 : (k + 1) * CH, :] for k in range(spans)], axis=0
        )
        full = jnp.sum(tots, axis=0, keepdims=True)
        tots = jnp.concatenate([tots] + [full] * (8 - spans), axis=0)
        wide = sum(dot(p, matrix) for p in pieces(tots, 3))
        adjoint = None
        for k in reversed(range(spans)):
            at = slice(k * CH, (k + 1) * CH)
            scale = spread(jnp.exp(cum_ref[at, :]), matrix)
            fresh = dot_rows(outof[at, :], (scale * rounded[at].astype(F32)).astype(BF16))
            adjoint = fresh if adjoint is None else jnp.exp(wide[k : k + 1]) * adjoint + fresh
            if k > 0:
                leaves[k - 1] = adjoint.astype(BF16)
        packed[:n, :] = adjoint.astype(BF16)
        packed[n:, :] = pack_tail(wide[spans : spans + 1], part)

    return kernel


def grad_partial_body(plan, g):
    spans, heads, part, pw = plan.spans, plan.heads, plan.part, plan.head_width

    def kernel(flipped, grad, leaves, into, cum_ref, step, skip, partial):
        cols = lax.broadcasted_iota(jnp.int32, (CH, CH), 1)
        left = cols < pw
        zero = jnp.zeros((CH, CH), BF16)
        matrix = spread_matrix(heads, part, g * plan.group_heads, pw)
        skip_wide = spread(jnp.broadcast_to(skip[...], (8, heads)), matrix)[0:1]
        for k in range(spans):
            at = slice(k * CH, (k + 1) * CH)
            cum = cum_ref[at, :]
            rest = skip_wide * grad[at, :].astype(F32)
            if k + 1 < spans:
                rate = jnp.exp(cum[CH - 1 : CH] - cum) * step[at, :]
                rest += spread(rate, matrix) * dot(into[at, :], leaves[k])
            for pair in range(plan.group_heads // 2):
                lanes = slice(pair * 2 * pw, (pair + 1) * 2 * pw)
                where = (g * plan.group_heads // 2 + pair) * 2 * CH
                x = grad[at, lanes]
                stacked = jnp.concatenate(
                    [jnp.where(left, x, zero), jnp.where(left, zero, x)], axis=0
                )
                partial[at, lanes] = (
                    dot(flipped[at, where : where + 2 * CH], stacked) + rest[:, lanes]
                )

    return kernel


def merge_body(plan, bit, first, last, reverse):
    n = plan.state

    def kernel(own, got, *refs):
        if first:
            outs = refs
        else:
            enter_in, decay_in = refs[:2]
            outs = refs[2:]
        enter_out, decay_out, packed = outs
        here = lax.axis_index("seq")
        high = ((here >> bit) & 1) == 1
        before = high != reverse
        flag = jnp.where(before, 1.0, 0.0)
        log_own, log_got = unpack_tail(own, n), unpack_tail(got, n)
        s_own, s_got = own[:n, :].astype(F32), got[:n, :].astype(F32)
        if first:
            enter_out[...] = flag * s_got
            decay_out[...] = flag * jnp.broadcast_to(log_got, decay_out.shape)
        else:
            scale = flag * jnp.exp(decay_in[0:1, :])
            enter_out[...] = enter_in[...] + scale * s_got
            decay_out[...] = decay_in[...] + flag * log_got
        pass_own = jnp.where(before, 1.0, jnp.exp(log_got))
        pass_got = jnp.where(before, jnp.exp(log_own), 1.0)
        packed[:n, :] = (pass_own * s_own + pass_got * s_got).astype(BF16)
        packed[n:, :] = pack_tail(log_own + log_got, plan.part)

    return kernel


def last_body(plan, g, bit, first, reverse):
    spans, heads, part, n = plan.spans, plan.heads, plan.part, plan.state

    def kernel(got, *refs):
        if first:
            rest = refs
        else:
            enter_in, decay_in = refs[:2]
            rest = refs[2:]
        if reverse:
            partial, proj, cum_ref, step, out = rest[0], rest[1], rest[2], rest[3], rest[-1]
        else:
            partial, proj, cum_ref, out = rest
        here = lax.axis_index("seq")
        high = ((here >> bit) & 1) == 1
        flag = jnp.where(high != reverse, 1.0, 0.0)
        s_got = got[:n, :].astype(F32)
        if first:
            enter = flag * s_got
        else:
            enter = enter_in[...] + flag * jnp.exp(decay_in[0:1, :]) * s_got
        high_part, low_part = pieces(enter, 2)
        matrix = spread_matrix(heads, part, g * plan.group_heads, plan.head_width)
        cum, total = device_cum(cum_ref, spans)
        if reverse:
            scale = jnp.exp(total - cum) * step[...]
        else:
            scale = jnp.exp(cum)
        through = dot(proj[...], high_part) + dot(proj[...], low_part)
        out[...] = (partial[...] + spread(scale, matrix) * through).astype(BF16)

    return kernel


def message_body(plan):
    def kernel(mat, ssd, out):
        out[...] = dot(mat[...], ssd[...]) + ssd[...].astype(F32)

    return kernel


def layer_body(plan, sides):
    def kernel(own, *refs):
        mats, parts, out = refs[:sides], refs[sides : 2 * sides], refs[-1]
        total = own[...]
        for s in range(sides):
            total += dot(mats[s][...], parts[s][...])
        out[...] = total.astype(BF16)

    return kernel


def shards(
    features,
    step_sizes,
    log_decay,
    state_in,
    state_out,
    skip_gain,
    kernels,
    edge_lists,
    edge_counts,
    cotangent,
):
    _, tok, width = features.shape
    heads = step_sizes.shape[2]
    n = state_in.shape[2]
    plan = Plan(tok, width, heads, n)
    part, groups, spans = plan.part, plan.groups, plan.spans
    bands = lax.axis_size("eta")
    segs = lax.axis_size("seq")
    rounds = segs.bit_length() - 1
    assert segs == 1 << rounds and rounds > 0
    feat, step, log = features[0], step_sizes[0], log_decay[0]
    into, outof, cot = state_in[0], state_out[0], cotangent[0]
    skip = skip_gain[None, :]

    if bands == 2:
        routes = [[(0, 1), (1, 0)]]
    elif bands > 2:
        routes = [
            [(i, (i + 1) % bands) for i in range(bands)],
            [(i, (i - 1) % bands) for i in range(bands)],
        ]
    else:
        routes = []
    sides = len(routes)

    def across(x, name):
        out = []
        for s, route in enumerate(routes):
            with jax.named_scope(f"{name}_{s}"):
                out.append(lax.ppermute(x, "eta", route))
        return out

    def swap(x, bit, name):
        with jax.named_scope(name):
            return lax.ppermute(x, "seq", [(i, i ^ (1 << bit)) for i in range(segs)])

    lanes = [slice(g * part, (g + 1) * part) for g in range(groups)]
    cot_far = [across(cot[:, lanes[g]], f"xcot{g}") for g in range(groups)]

    res = run(
        states_body(plan),
        [shape((tok, heads), F32)]
        + [shape((spans - 1, n, part), BF16), shape((n + PAD, part), BF16)] * groups,
        (feat, step, log, into),
        us=4,
        name="states",
    )
    cum, prefixes, packs = res[0], res[1::2], res[2::2]

    def scan_rounds(packed, tag, reverse, g):
        carry = ()
        for bit in range(rounds):
            got = swap(packed, bit, f"z{tag}{g}r{bit}")
            if bit == rounds - 1:
                return got, carry
            enter, decay, packed = run(
                merge_body(plan, bit, bit == 0, False, reverse),
                [shape((n, part), F32), shape((8, part), F32), shape((n + PAD, part), BF16)],
                (packed, got, *carry),
                name=f"merge_{tag}{g}",
            )
            carry = (enter, decay)

    ready = [scan_rounds(packs[g], "f", False, g) for g in range(groups)]

    smem = pl.BlockSpec(memory_space=pltpu.SMEM)
    vmem = pl.BlockSpec(memory_space=pltpu.VMEM)
    square = shape((tok, tok), BF16)
    res = run(
        graph_body(plan, sides),
        [square] * (1 + 2 * sides) + [shape((tok, part), F32)] * groups,
        (edge_lists, edge_counts, kernels, cot),
        in_specs=[smem, smem, vmem, vmem],
        scratch_shapes=[pltpu.VMEM((tok, tok), BF16)],
        us=4,
        name="graph",
    )
    fwd_own, fwd_side, back_side = res[0], res[1 : 1 + sides], res[1 + sides : 1 + 2 * sides]
    own_back = res[1 + 2 * sides :]

    res = run(
        weights_body(plan),
        [shape((tok, heads * CH), BF16)] + [shape((tok, part), F32)] * groups,
        (feat, step, cum, into, outof, skip, *prefixes),
        us=8,
        name="weights",
    )
    flipped, partials = res[0], res[1:]

    grads, leaves, back_ready = [], [], []
    for g in range(groups):
        grad, leave, packed = run(
            grad_body(plan, sides, g),
            [shape((tok, part), BF16), shape((spans - 1, n, part), BF16), shape((n + PAD, part), BF16)],
            (own_back[g], cum, outof, *back_side, *cot_far[g]),
            us=3,
            name=f"grad{g}",
        )
        grads.append(grad)
        leaves.append(leave)
        back_ready.append(scan_rounds(packed, "b", True, g))

    ssds, ssd_far = [], []
    for g in range(groups):
        got, carry = ready[g]
        ssd = run(
            last_body(plan, g, rounds - 1, rounds == 1, False),
            shape((tok, part), BF16),
            (got, *carry, partials[g], outof, cum),
            us=2,
            name=f"ssd{g}",
        )
        ssds.append(ssd)
        ssd_far.append(across(ssd, f"xssd{g}"))

    owns = [
        run(message_body(plan), shape((tok, part), F32), (fwd_own, ssds[g]), us=2, name=f"own{g}")
        for g in range(groups)
    ]

    def placed(kernel, args, g, held, us, name):
        full = lambda a: pl.BlockSpec(a.shape, lambda i, nd=a.ndim: (0,) * nd)
        specs = [full(a) for a in args]
        aliases = {}
        if held is not None:
            aliases = {len(args): 0}
            args = (*args, held)
            specs.append(pl.BlockSpec(memory_space=pl.ANY))
        return run(
            kernel,
            shape((tok, width), BF16),
            args,
            in_specs=specs,
            out_specs=pl.BlockSpec((tok, part), lambda i, g=g: (0, g)),
            aliases=aliases,
            us=us,
            name=name,
            grid=(1,),
        )

    grad_out = None
    for g in range(groups):
        grad_partial = run(
            grad_partial_body(plan, g),
            shape((tok, part), F32),
            (flipped, grads[g], leaves[g], into, cum, step, skip),
            us=3,
            name=f"gradp{g}",
        )
        got, carry = back_ready[g]
        grad_out = placed(
            last_body(plan, g, rounds - 1, rounds == 1, True),
            (got, *carry, grad_partial, into, cum, step),
            g,
            grad_out,
            2,
            f"gradf{g}",
        )

    layer_out = None
    for g in range(groups):
        layer_out = placed(
            layer_body(plan, sides), (owns[g], *fwd_side, *ssd_far[g]), g, layer_out, 2, f"layer{g}"
        )

    return layer_out[None], grad_out[None]


def solution(mesh):
    return jax.shard_map(
        shards,
        mesh=mesh,
        in_specs=(
            P(("groups", "eta"), "seq", "rep"),
            P(("groups", "eta"), "seq", "rep"),
            P(("groups", "eta"), "seq", "rep"),
            P(("groups", "eta"), "seq", None),
            P(("groups", "eta"), "seq", None),
            P("rep"),
            P(),
            P("groups", "seq", None, None),
            P("groups", "seq"),
            P(("groups", "eta"), "seq", "rep"),
        ),
        out_specs=(P(("groups", "eta"), "seq", "rep"), P(("groups", "eta"), "seq", "rep")),
        check_vma=False,
    )
```

```python
import jax
import jax.numpy as jnp
from jax import lax
from jax.experimental import pallas as pl
from jax.experimental.pallas import tpu as pltpu
from jax.sharding import PartitionSpec as P


CH = 128
BLOCK = 128
TYPES = 4
PAD = 16
GROUPS = 2
COT_CUTS = ((1, 3), (1,))
SSD_CUTS = ((1,), (3, 1))
VMEM = 8 << 20


F32 = jnp.float32
BF16 = jnp.bfloat16


def dot(a, b):
    return jnp.dot(a, b, preferred_element_type=F32)


def dot_rows(a, b):
    return lax.dot_general(a, b, (((0,), (0,)), ((), ())), preferred_element_type=F32)


def pieces(x, count):
    out = []
    for _ in range(count):
        part = x.astype(BF16)
        out.append(part)
        x = x - part.astype(F32)
    return out


def spread_matrix(heads, width, first, head_width):
    row = lax.broadcasted_iota(jnp.int32, (heads, width), 0)
    col = lax.broadcasted_iota(jnp.int32, (heads, width), 1)
    low = (row - first) * head_width
    return ((col >= low) & (col < low + head_width)).astype(F32).astype(BF16)


def spread(x, matrix):
    high, low = pieces(x, 2)
    return dot_rows(high, matrix) + dot_rows(low, matrix)


def spread_row(x, matrix):
    wide = jnp.broadcast_to(x, (8, x.shape[1]))
    return sum(dot(p, matrix) for p in pieces(wide, 3))[0:1]


def run(kernel, outs, args, in_specs=None, out_specs=None, aliases=None, us=1.0, **kw):
    vmem = pl.BlockSpec(memory_space=pltpu.VMEM)
    return pl.pallas_call(
        kernel,
        out_shape=outs,
        in_specs=in_specs or [vmem] * len(args),
        out_specs=out_specs or jax.tree.map(lambda _: vmem, outs),
        input_output_aliases=aliases or {},
        cost_estimate=pl.CostEstimate(
            flops=0, bytes_accessed=int(us * 3.0e6), transcendentals=0
        ),
        compiler_params=pltpu.CompilerParams(vmem_limit_bytes=VMEM),
        **kw,
    )(*args)


def shape(dims, kind):
    return jax.ShapeDtypeStruct(dims, kind)


class Plan:
    def __init__(self, tok, width, heads, state):
        self.tok, self.width, self.heads, self.state = tok, width, heads, state
        self.head_width = width // heads
        self.spans = tok // CH
        self.groups = GROUPS
        self.part = width // GROUPS
        self.group_heads = heads // GROUPS


def pack_tail(total, part):
    tail = jnp.concatenate([p.astype(F32) for p in pieces(total, 3)], axis=0)
    return jnp.concatenate([tail, jnp.zeros((PAD - 3, part), F32)], axis=0).astype(BF16)


def unpack_tail(ref, rows):
    tail = ref[rows : rows + PAD, :].astype(F32)
    return tail[0:1] + tail[1:2] + tail[2:3]


def cuts(table, part):
    out = []
    for shares in table:
        unit, low, ranges = part // sum(shares), 0, []
        for share in shares:
            ranges.append(slice(low, low + share * unit))
            low += share * unit
        out.append(ranges)
    return out


def totals(cum_ref, matrix, spans):
    ends = [cum_ref[:, (k + 1) * CH - 1 : (k + 1) * CH] for k in range(spans)]
    lane = lax.broadcasted_iota(jnp.int32, (cum_ref.shape[0], CH), 1)
    table = jnp.where(lane == spans, sum(ends), 0.0)
    for k, end in enumerate(ends):
        table = jnp.where(lane == k, end, table)
    return sum(dot_rows(p, matrix) for p in pieces(table, 3))


def states_body(plan, g):
    spans, heads, part, n = plan.spans, plan.heads, plan.part, plan.state
    lanes = slice(g * part, (g + 1) * part)

    def kernel(feat, step, log, into, skip, kern, *outs):
        if g == 0:
            cum_ref, prefix_out, packed = outs
            rows = lax.broadcasted_iota(jnp.int32, (CH, CH), 0)
            cols = lax.broadcasted_iota(jnp.int32, (CH, CH), 1)
            upper = (rows <= cols).astype(F32).astype(BF16)
            for k in range(spans):
                at = slice(k * CH, (k + 1) * CH)
                cum_ref[:, at] = sum(dot(p, upper) for p in pieces(log[:, at], 3))
        else:
            cum_ref, (prefix_out, packed) = log, outs
        matrix = spread_matrix(heads, part, g * plan.group_heads, plan.head_width)
        tot_wide = totals(cum_ref, matrix, spans)
        state = None
        for k in range(spans):
            at = slice(k * CH, (k + 1) * CH)
            cum = cum_ref[:, at]
            rate = jnp.exp(cum[:, CH - 1 : CH] - cum) * step[:, at]
            scaled = (spread(rate, matrix) * feat[at, lanes].astype(F32)).astype(BF16)
            fresh = dot_rows(into[at, :], scaled)
            state = fresh if state is None else jnp.exp(tot_wide[k : k + 1]) * state + fresh
            if k + 1 < spans:
                prefix_out[k] = state.astype(BF16)
        packed[:n, :] = state.astype(BF16)
        packed[n:, :] = pack_tail(tot_wide[spans : spans + 1], part)

    return kernel


def weights_body(plan, g):
    spans, heads, part, pw = plan.spans, plan.heads, plan.part, plan.head_width

    def kernel(feat, step, cum_ref, into, outof, skip, prefix, flipped, partial):
        rows = lax.broadcasted_iota(jnp.int32, (CH, CH), 0)
        cols = lax.broadcasted_iota(jnp.int32, (CH, CH), 1)
        causal = rows >= cols
        left = cols < pw
        zero = jnp.zeros((CH, CH), BF16)
        base = g * part
        matrix = spread_matrix(heads, part, g * plan.group_heads, pw)
        skip_wide = spread_row(skip[...], matrix)
        for k in range(spans):
            at = slice(k * CH, (k + 1) * CH)
            score = lax.dot_general(
                outof[at, :], into[at, :], (((1,), (1,)), ((), ())), preferred_element_type=F32
            )
            score = jnp.where(causal, score, 0.0)
            cum = cum_ref[:, at]
            turned = jnp.concatenate([cum, jnp.zeros((CH - heads, CH), F32)], axis=0).T
            rest = skip_wide * feat[at, base : base + part].astype(F32)
            if k > 0:
                rest += spread(jnp.exp(cum), matrix) * dot(outof[at, :], prefix[k - 1])
            for pair in range(plan.group_heads // 2):
                lanes = slice(pair * 2 * pw, (pair + 1) * 2 * pw)
                ws = []
                for h in (0, 1):
                    head = g * plan.group_heads + 2 * pair + h
                    gap = turned[:, head : head + 1] - cum[head : head + 1, :]
                    decay = jnp.exp(jnp.minimum(gap, 0.0))
                    w = (score * decay * step[head : head + 1, at]).astype(BF16)
                    ws.append(w)
                    flipped[at, (2 * pair + h) * CH : (2 * pair + h + 1) * CH] = w.T
                x = feat[at, base + pair * 2 * pw : base + (pair + 1) * 2 * pw]
                stacked = jnp.concatenate(
                    [jnp.where(left, x, zero), jnp.where(left, zero, x)], axis=0
                )
                inside = dot(jnp.concatenate(ws, axis=1), stacked)
                partial[at, lanes] = inside + rest[:, lanes]

    return kernel


def cut_body(lanes):
    def kernel(whole, out, sem):
        copy = pltpu.make_async_copy(whole.at[:, lanes], out, sem)
        copy.start()
        copy.wait()

    return kernel


def device_cum(cum_ref, spans):
    out, before = [], None
    for k in range(spans):
        cum = cum_ref[:, k * CH : (k + 1) * CH]
        out.append(cum if before is None else cum + before)
        before = out[-1][:, CH - 1 : CH]
    return jnp.concatenate(out, axis=1), before


def graph_body(plan, sides, slots):
    tok = plan.tok
    spare = (1 + sides) * tok

    def kernel(edges, counts, kern, *refs):
        ranges = cuts(COT_CUTS, plan.part)
        pieces_in = sum(len(r) for r in ranges)
        cots, refs = refs[:pieces_in], refs[pieces_in:]
        ahead, back = refs[:2]
        own_back, flipped = refs[2:-1], refs[-1]
        bands = lax.axis_size("eta")
        band = lax.axis_index("eta")
        for ref in (ahead, back):
            ref[:spare, :] = jnp.zeros((spare, tok), BF16)
        for t in range(kern.shape[0]):
            flipped[t] = kern[t].T

        def spot(live, panel, a, b):
            row = jnp.where(live, panel * tok + a * BLOCK, spare)
            return (
                pl.ds(pl.multiple_of(row, BLOCK), BLOCK),
                pl.ds(pl.multiple_of(b * BLOCK, BLOCK), BLOCK),
            )

        if sides == 1:
            offsets, others = [2 - 2 * band], [1 - band]
        else:
            offsets, others = [0, 2][:sides], [band - 1, band + 1][:sides]

        def read(owner, e):
            off, src, dst, kind = (edges[owner, 0, f, e] for f in range(4))
            return off, src & (tok // BLOCK - 1), dst & (tok // BLOCK - 1), kind & (TYPES - 1)

        for e in range(slots):
            off, src, dst, kind = read(band, e)
            live = e < counts[0, band]
            panel = jnp.where(off == 1, 0, 1)
            if sides > 1:
                panel = jnp.where(off == 2, 2, panel)
            ahead[spot(live, panel, dst, src)] = kern[kind]
            back[spot(live & (off == 1), 0, src, dst)] = flipped[kind]
        for s in range(sides):
            real = (others[s] >= 0) & (others[s] < bands)
            other = jnp.clip(others[s], 0, bands - 1)
            for e in range(slots):
                off, src, dst, kind = read(other, e)
                live = real & (e < counts[0, other]) & (off == 2 - offsets[s])
                back[spot(live, 1 + s, src, dst)] = flipped[kind]
        spots = [(g, lanes) for g in range(plan.groups) for lanes in ranges[g]]
        for (g, lanes), ref in zip(spots, cots):
            cot = ref[...]
            own_back[g][:, lanes] = dot(back[:tok, :], cot) + cot.astype(F32)

    return kernel


def grad_body(plan, sides, g):
    spans, heads, part, n = plan.spans, plan.heads, plan.part, plan.state

    def kernel(own_back, cum_ref, outof, mats, *refs):
        cots = refs[:-3]
        grad, leaves, packed = refs[-3:]
        ranges = cuts(COT_CUTS, part)[g]
        matrix = spread_matrix(heads, part, g * plan.group_heads, plan.head_width)
        total = own_back[...]
        for s in range(sides):
            panel = mats[(1 + s) * plan.tok : (2 + s) * plan.tok, :]
            far = [dot(panel, cots[i * sides + s][...]) for i in range(len(ranges))]
            total += far[0] if len(far) == 1 else jnp.concatenate(far, axis=1)
        rounded = total.astype(BF16)
        grad[...] = rounded
        wide = totals(cum_ref, matrix, spans)
        adjoint = None
        for k in reversed(range(spans)):
            at = slice(k * CH, (k + 1) * CH)
            scale = spread(jnp.exp(cum_ref[:, at]), matrix)
            fresh = dot_rows(outof[at, :], (scale * rounded[at].astype(F32)).astype(BF16))
            adjoint = fresh if adjoint is None else jnp.exp(wide[k : k + 1]) * adjoint + fresh
            if k > 0:
                leaves[k - 1] = adjoint.astype(BF16)
        packed[:n, :] = adjoint.astype(BF16)
        packed[n:, :] = pack_tail(wide[spans : spans + 1], part)

    return kernel


def grad_partial_body(plan, g):
    spans, heads, part, pw = plan.spans, plan.heads, plan.part, plan.head_width

    def kernel(flipped, grad, leaves, into, cum_ref, step, skip, partial):
        cols = lax.broadcasted_iota(jnp.int32, (CH, CH), 1)
        left = cols < pw
        zero = jnp.zeros((CH, CH), BF16)
        matrix = spread_matrix(heads, part, g * plan.group_heads, pw)
        skip_wide = spread_row(skip[...], matrix)
        for k in range(spans):
            at = slice(k * CH, (k + 1) * CH)
            cum = cum_ref[:, at]
            rest = skip_wide * grad[at, :].astype(F32)
            if k + 1 < spans:
                rate = jnp.exp(cum[:, CH - 1 : CH] - cum) * step[:, at]
                rest += spread(rate, matrix) * dot(into[at, :], leaves[k])
            for pair in range(plan.group_heads // 2):
                lanes = slice(pair * 2 * pw, (pair + 1) * 2 * pw)
                where = pair * 2 * CH
                x = grad[at, lanes]
                stacked = jnp.concatenate(
                    [jnp.where(left, x, zero), jnp.where(left, zero, x)], axis=0
                )
                partial[at, lanes] = (
                    dot(flipped[at, where : where + 2 * CH], stacked) + rest[:, lanes]
                )

    return kernel


def merge_body(plan, bit, last, mixed, reverse):
    n = plan.state

    def kernel(own, got, *refs):
        enter_out, decay_out, packed = refs[-3:]
        here = lax.axis_index("seq")
        high = ((here >> bit) & 1) == 1
        before = high != reverse
        flag = jnp.where(before, 1.0, 0.0)
        log_own, log_got = unpack_tail(own, n), unpack_tail(got, n)
        s_own, s_got = own[:n, :].astype(F32), got[:n, :].astype(F32)
        if bit == 0:
            enter_out[...] = flag * s_got
            decay_out[...] = flag * jnp.broadcast_to(log_got, decay_out.shape)
        else:
            enter_in, decay_in = refs[:2]
            scale = flag * jnp.exp(decay_in[0:1, :])
            enter_out[...] = enter_in[...] + scale * s_got
            decay_out[...] = decay_in[...] + flag * log_got
        pass_own = jnp.where(before, 1.0, jnp.exp(log_got))
        pass_got = jnp.where(before, jnp.exp(log_own), 1.0)
        packed[:n, :] = (pass_own * s_own + pass_got * s_got).astype(BF16)
        packed[n:, :] = pack_tail(log_own + log_got, plan.part)
        if mixed:

            @pl.when(((here >> last) & 1) == 0)
            def _():
                packed[...] = refs[-4][...]

    return kernel


def store(write, out, lanes, scratch, sems):
    copies = []
    for k in range(sems.shape[0]):
        rows = slice(k * CH, (k + 1) * CH)
        scratch[rows, :] = write(rows).astype(BF16)
        copies.append(pltpu.make_async_copy(scratch.at[rows, :], out.at[rows, lanes], sems.at[k]))
        copies[-1].start()
    for copy in copies:
        copy.wait()


def last_body(plan, g, bit, reverse):
    spans, heads, part = plan.spans, plan.heads, plan.part
    n = plan.state

    def kernel(got, enter_in, decay_in, *rest):
        partial, proj, cum_ref = rest[:3]
        here = lax.axis_index("seq")
        high = ((here >> bit) & 1) == 1
        flag = jnp.where(high != reverse, 1.0, 0.0)
        enter = enter_in[...] + flag * jnp.exp(decay_in[0:1, :]) * got[:n, :].astype(F32)
        high_part, low_part = pieces(enter, 2)
        matrix = spread_matrix(heads, part, g * plan.group_heads, plan.head_width)
        cum, total = device_cum(cum_ref, spans)
        if reverse:
            scale = jnp.exp(total - cum) * rest[3][...]
        else:
            scale = jnp.exp(cum)

        def write(rows):
            through = dot(proj[rows, :], high_part) + dot(proj[rows, :], low_part)
            return partial[rows, :] + spread(scale[:, rows], matrix) * through

        if reverse:
            out, scratch, sems = rest[-3:]
            store(write, out, slice(g * part, (g + 1) * part), scratch, sems)
        else:
            for k in range(spans):
                rows = slice(k * CH, (k + 1) * CH)
                value = write(rows).astype(BF16)
                for ref, lanes in zip(rest[3:], cuts(SSD_CUTS, part)[g]):
                    ref[rows, :] = value[:, lanes]

    return kernel


def message_body(plan, g):
    def kernel(mat, *refs):
        out = refs[-1]
        for ssd, lanes in zip(refs[:-1], cuts(SSD_CUTS, plan.part)[g]):
            out[:, lanes] = dot(mat[: plan.tok, :], ssd[...]) + ssd[...].astype(F32)

    return kernel


def layer_body(plan, sides, g, lanes):
    tok = plan.tok

    def kernel(own, mats, *refs):
        parts = refs[:sides]
        out, scratch, sems = refs[-3:]

        def write(rows):
            total = own[rows, lanes]
            for s in range(sides):
                first = (1 + s) * tok + rows.start
                total += dot(mats[first : first + CH, :], parts[s][...])
            return total

        base = g * plan.part
        store(write, out, slice(base + lanes.start, base + lanes.stop), scratch, sems)

    return kernel


def shards(
    features,
    step_sizes,
    log_decay,
    state_in,
    state_out,
    skip_gain,
    kernels,
    edge_lists,
    edge_counts,
    cotangent,
):
    _, tok, width = features.shape
    heads = step_sizes.shape[2]
    n = state_in.shape[2]
    plan = Plan(tok, width, heads, n)
    part, groups, spans = plan.part, plan.groups, plan.spans
    bands = lax.axis_size("eta")
    segs = lax.axis_size("seq")
    rounds = segs.bit_length() - 1
    assert segs == 1 << rounds and rounds > 1
    feat, step, log = features[0], step_sizes[0].T, log_decay[0].T
    edges, counts = jnp.swapaxes(edge_lists, 2, 3), edge_counts.T
    into, outof, cot = state_in[0], state_out[0], cotangent[0]
    skip = skip_gain[None, :]

    if bands == 2:
        routes = [[(0, 1), (1, 0)]]
    elif bands > 2:
        routes = [
            [(i, (i + 1) % bands) for i in range(bands)],
            [(i, (i - 1) % bands) for i in range(bands)],
        ]
    else:
        routes = []
    sides = len(routes)

    def across(x):
        out = []
        for route in routes:
            out.append(lax.ppermute(x, "eta", route))
        return out

    def swap(x, bit):
        return lax.ppermute(x, "seq", [(i, i ^ (1 << bit)) for i in range(segs)])

    smem = pl.BlockSpec(memory_space=pltpu.SMEM)
    vmem = pl.BlockSpec(memory_space=pltpu.VMEM)
    cots, cot_far = [], []
    for g in range(groups):
        cot_far.append([])
        for i, at in enumerate(cuts(COT_CUTS, part)[g]):
            held = g * part + at.start
            if g == i == 0:
                piece = cot[:, : at.stop]
            else:
                piece = run(
                    cut_body(slice(held, held + at.stop - at.start)),
                    shape((tok, at.stop - at.start), BF16),
                    (cot,),
                    in_specs=[pl.BlockSpec(memory_space=pltpu.HBM)],
                    scratch_shapes=[pltpu.SemaphoreType.DMA],
                )
            cots.append(piece)
            cot_far[g] += across(piece)

    cum, prefixes, packs = None, [], []
    for g in range(groups):
        res = run(
            states_body(plan, g),
            [shape((heads, tok), F32)] * (g == 0)
            + [shape((spans - 1, n, part), BF16), shape((n + PAD, part), BF16)],
            (feat, step, log if g == 0 else cum, into, skip, kernels),
            us=2,
        )
        cum = res[0] if g == 0 else cum
        prefixes.append(res[-2])
        packs.append(res[-1])

    def scan_rounds(packed, reverse, other=None):
        carry = ()
        for bit in range(rounds - 1):
            got = swap(packed, bit)
            extra = () if other is None or bit < rounds - 2 else (other,)
            enter, decay, packed = run(
                merge_body(plan, bit, rounds - 1, bool(extra), reverse),
                [shape((n, part), F32), shape((8, part), F32), shape((n + PAD, part), BF16)],
                (packed, got, *carry, *extra),
            )
            carry = (enter, decay)
        return packed, carry

    def finish(packed):
        return swap(packed, rounds - 1)

    packed, carry = scan_rounds(packs[0], False)
    ready = [(finish(packed), carry)]
    fwd_packed, fwd_carry = scan_rounds(packs[1], False)

    tiles = shape(((1 + sides) * tok + BLOCK, tok), BF16)
    res = run(
        graph_body(plan, sides, edge_lists.shape[2]),
        [tiles, tiles] + [shape((tok, part), F32)] * groups,
        (edges, counts, kernels, *cots),
        in_specs=[smem, smem, vmem] + [vmem] * len(cots),
        scratch_shapes=[pltpu.VMEM(kernels.shape, BF16)],
        us=2,
    )
    ahead, back, own_back = res[0], res[1], res[2:]

    flipped, partials = [], []
    for g in range(groups):
        turned, partial = run(
            weights_body(plan, g),
            [shape((tok, plan.group_heads * CH), BF16), shape((tok, part), F32)],
            (feat, step, cum, into, outof, skip, prefixes[g]),
            us=3,
        )
        flipped.append(turned)
        partials.append(partial)

    grads, leaves, back_ready = [], [], []
    for g in range(groups):
        grad, leave, packed = run(
            grad_body(plan, sides, g),
            [shape((tok, part), BF16), shape((spans - 1, n, part), BF16), shape((n + PAD, part), BF16)],
            (own_back[g], cum, outof, back, *cot_far[g]),
            us=2,
        )
        grads.append(grad)
        leaves.append(leave)
        if g == 0:
            packed, carry = scan_rounds(packed, True, fwd_packed)
            got = finish(packed)
            ready.append((got, fwd_carry))
        else:
            packed, carry = scan_rounds(packed, True)
            got = finish(packed)
        back_ready.append((got, carry))

    ssds, ssd_far = [], []
    ssd_cuts = cuts(SSD_CUTS, part)
    for g in range(groups):
        got, carry = ready[g]
        ssd = run(
            last_body(plan, g, rounds - 1, False),
            [shape((tok, at.stop - at.start), BF16) for at in ssd_cuts[g]],
            (got, *carry, partials[g], outof, cum),
            us=1,
        )
        ssds.append(ssd)
        ssd_far.append([across(piece) for piece in ssd])

    owns = [
        run(message_body(plan, g), shape((tok, part), F32), (ahead, *ssds[g]), us=1)
        for g in range(groups)
    ]

    def placed(kernel, args, span, held):
        specs = [vmem] * len(args)
        aliases = {}
        if held is not None:
            aliases = {len(args): 0}
            args = (*args, held)
            specs.append(pl.BlockSpec(memory_space=pl.ANY))
        return run(
            kernel,
            shape((tok, width), BF16),
            args,
            in_specs=specs,
            out_specs=pl.BlockSpec(memory_space=pl.ANY),
            aliases=aliases,
            us=2,
            scratch_shapes=[pltpu.VMEM((tok, span), BF16), pltpu.SemaphoreType.DMA((tok // CH,))],
        )

    grad_out = None
    for g in range(groups):
        grad_partial = run(
            grad_partial_body(plan, g),
            shape((tok, part), F32),
            (flipped[g], grads[g], leaves[g], into, cum, step, skip),
            us=1,
        )
        got, carry = back_ready[g]
        grad_out = placed(
            last_body(plan, g, rounds - 1, True),
            (got, *carry, grad_partial, into, cum, step),
            part,
            grad_out,
        )

    layer_out = None
    for g in range(groups):
        for i, at in enumerate(ssd_cuts[g]):
            layer_out = placed(
                layer_body(plan, sides, g, at),
                (owns[g], ahead, *ssd_far[g][i]),
                at.stop - at.start,
                layer_out,
            )

    return layer_out[None], grad_out[None]


def solution(mesh):
    return jax.shard_map(
        shards,
        mesh=mesh,
        in_specs=(
            P(("groups", "eta"), "seq", "rep"),
            P(("groups", "eta"), "seq", "rep"),
            P(("groups", "eta"), "seq", "rep"),
            P(("groups", "eta"), "seq", None),
            P(("groups", "eta"), "seq", None),
            P("rep"),
            P(),
            P("groups", "seq", None, None),
            P("groups", "seq"),
            P(("groups", "eta"), "seq", "rep"),
        ),
        out_specs=(P(("groups", "eta"), "seq", "rep"), P(("groups", "eta"), "seq", "rep")),
        check_vma=False,
    )
```
